256 devices in a mesh: samp: 8 (over y, core), feat: 32 (over x, z).
Axes of the slice: x: 4, y: 4, z: 8, core: 2. Of those that a mesh axis runs over, the one named last changes fastest.
Arguments:
- samples: bfloat16 [8192, 16384], P('samp', 'feat'), may hold values from -8 to 8
- precision: float32 [128, 8, 128, 128], P('feat'), may hold values from -1.2 to 2
- col_blocks: int32 [128, 8], P('feat'), may hold values from -1 to 127, as said below
Outputs:
- updated: float32 [128, 8, 128, 128], P('feat')
The draws below stay inside these ranges and needn't reach their ends.
Inputs may be any that keep to these rules, and one draw needn't show every extreme that they name: `col_blocks`: slot 0 of block row j holds j; the other column blocks of a row follow in increasing order, then -1 fills the empty slots. The pattern is symmetric: row j names c exactly when row c names j. Block row j lies on index j // 4 of feat; for two different such indices, at most one block row of the one names a column block of the other, and the block rows of one index name column blocks of at most 16 other indices.
All inputs are finite; a program needn't handle non-finite values.
Results may differ from the reference program's by a relative error of at most 0.0028.
Values may be sent and summed in bfloat16 or wider, within the bound.
A program may use at most 128 MiB of HBM per device.

```python
import jax
import jax.numpy as jnp
from jax import lax

BLOCK = 128
BR_DEV = 4
ITERS = 3
SPAN = 8
MAXB = 8
NB = 128
FEATURES = 16384
SAMPLES = 8192


def block_pattern(key):
    device_count = NB // BR_DEV
    reach_count = SPAN
    perm_key, rot_key, edge_key, pair_key = jax.random.split(key, 4)
    ordering = jax.random.permutation(perm_key, device_count)
    rotate = jax.random.randint(rot_key, (device_count,), 0, BR_DEV)
    labels = jnp.arange(device_count)
    offsets = jnp.arange(1, reach_count + 1)
    chosen = jax.random.randint(edge_key, (device_count, reach_count), 0, 2)
    forced = (labels[:, None] == 0) | (labels[:, None] == device_count - offsets[None, :])
    chosen = jnp.where(forced, 1, chosen)
    upper_end = (labels[:, None] + offsets[None, :]) % device_count
    lower_row = ordering[:, None] * BR_DEV + (offsets[None, :] + rotate[:, None]) % BR_DEV
    upper_row = ordering[upper_end] * BR_DEV + (offsets[None, :] + 2 + rotate[upper_end]) % BR_DEV
    adjacency = jnp.zeros((NB, NB), jnp.int32)
    adjacency = adjacency.at[lower_row.reshape(-1), upper_row.reshape(-1)].max(chosen.reshape(-1))
    adjacency = adjacency.at[upper_row.reshape(-1), lower_row.reshape(-1)].max(chosen.reshape(-1))
    pair_first = jnp.array([one for one in range(BR_DEV) for other in range(one + 1, BR_DEV)], jnp.int32)
    pair_second = jnp.array([other for one in range(BR_DEV) for other in range(one + 1, BR_DEV)], jnp.int32)
    inside = jax.random.randint(pair_key, (device_count, pair_first.shape[0]), 0, 6)
    inside = jnp.where(labels[:, None] == 0, 0, inside)
    picked = (inside == 0).astype(jnp.int32)
    rows_first = ordering[:, None] * BR_DEV + pair_first[None, :]
    rows_second = ordering[:, None] * BR_DEV + pair_second[None, :]
    adjacency = adjacency.at[rows_first.reshape(-1), rows_second.reshape(-1)].max(picked.reshape(-1))
    adjacency = adjacency.at[rows_second.reshape(-1), rows_first.reshape(-1)].max(picked.reshape(-1))
    col_ids = jnp.arange(NB)
    scores = jnp.where(col_ids[None, :] == col_ids[:, None], -1, jnp.where(adjacency > 0, col_ids[None, :], NB + col_ids[None, :]))
    ranked = jnp.argsort(scores, axis=1, stable=True)[:, :MAXB]
    present = (jnp.take_along_axis(adjacency, ranked, axis=1) > 0) | (ranked == col_ids[:, None])
    return jnp.where(present, ranked, -1).astype(jnp.int32)


def draw_col_blocks(key, part):
    return block_pattern(jax.random.fold_in(key, 11))


def draw_precision(key, part):
    pattern = block_pattern(jax.random.fold_in(key, 11))
    value_key, diag_key = jax.random.split(jax.random.fold_in(key, 12), 2)
    shape = (NB, MAXB, BLOCK, BLOCK)
    entries = jax.random.truncated_normal(value_key, -4.0, 4.0, shape, jnp.float32) * 0.3
    diagonal = jax.random.uniform(diag_key, (NB, 1, BLOCK, 1), jnp.float32, 1.0, 2.0)
    row_ids = jnp.arange(NB)[:, None]
    on_diagonal = (pattern == row_ids)[:, :, None, None] & jnp.eye(BLOCK, dtype=bool)[None, None]
    values = jnp.where(on_diagonal, diagonal, entries)
    return jnp.where((pattern >= 0)[:, :, None, None], values, 0.0).astype(jnp.float32)


def draw_samples(key, part):
    value_key, scale_key = jax.random.split(jax.random.fold_in(key, 13), 2)
    shape = (SAMPLES, FEATURES)
    scales = jnp.exp(jax.random.uniform(scale_key, (1, FEATURES), jnp.float32, -0.69, 0.69))
    base = jax.random.truncated_normal(value_key, -4.0, 4.0, shape, jnp.float32)
    return (base * scales).astype(jnp.bfloat16)


def setup_inputs(seed: int = 0) -> dict:
    key_of = jax.random.split(jax.random.key(seed), 4)
    return {
        "samples": draw_samples(jax.random.fold_in(key_of[3], 71), 0),
        "precision": draw_precision(jax.random.fold_in(key_of[3], 71), 0),
        "col_blocks": draw_col_blocks(jax.random.fold_in(key_of[3], 71), 0),
    }


step_size = 0.2
penalty = 0.25

def reference(samples, precision, col_blocks):
    sample_total = samples.shape[0]
    block_count = col_blocks.shape[0]
    slot_count = col_blocks.shape[1]
    block_size = precision.shape[2]
    filled = col_blocks >= 0
    safe_cols = jnp.where(filled, col_blocks, 0).astype(jnp.int32)
    xblocks = samples.reshape(sample_total, block_count, block_size)
    row_ids = jnp.arange(block_count, dtype=jnp.int32)
    identity_mask = jnp.eye(block_size, dtype=bool)
    on_diagonal = (col_blocks == row_ids[:, None])[:, :, None, None] & identity_mask[None, None]
    keep_mask = filled[:, :, None, None]
    matching = col_blocks[safe_cols] == row_ids[:, None, None]
    mate_slot = jnp.argmax(matching, axis=2).astype(jnp.int32)
    current = jnp.where(keep_mask, precision, jnp.float32(0.0))
    for iteration in range(ITERS):
        weights = current.astype(jnp.bfloat16)

        def row_terms(block_row):
            picked = jnp.take(xblocks, safe_cols[block_row], axis=1).reshape(sample_total, slot_count * block_size)
            weight_row = jnp.transpose(weights[block_row], (0, 2, 1)).reshape(slot_count * block_size, block_size)
            projected = jnp.dot(picked, weight_row, preferred_element_type=jnp.float32).astype(jnp.bfloat16)
            gram_row = jnp.dot(projected.T, picked, preferred_element_type=jnp.float32)
            return gram_row.reshape(block_size, slot_count, block_size).transpose(1, 0, 2)
        gram_blocks = lax.map(row_terms, row_ids) / sample_total
        mirror = gram_blocks[safe_cols, mate_slot]
        gradient = 0.5 * (gram_blocks + jnp.swapaxes(mirror, 2, 3))
        stepped = current - step_size * gradient
        shrunk = jnp.sign(stepped) * jnp.maximum(jnp.abs(stepped) - step_size * penalty, 0.0)
        rooted = 0.5 * (stepped + jnp.sqrt(stepped * stepped + 4.0 * step_size))
        current = jnp.where(keep_mask, jnp.where(on_diagonal, rooted, shrunk), jnp.float32(0.0))
    return current
```

```python
import functools

import jax
import jax.numpy as jnp
from jax import lax
from jax.experimental import pallas as pl
from jax.experimental.pallas import tpu as pltpu
from jax.sharding import PartitionSpec as P

ITERS = 3
STEP = 0.2
SHRINK = 0.2 * 0.25
NX, NZ, NY, NC = 4, 8, 4, 2
NS = NY * NC
NF = NX * NZ
BR, SL, BK = 4, 8, 128
NBK = BR * SL
CH = BK // NS
ROWS = 1024
F32, BF16 = jnp.float32, jnp.bfloat16
MESH = pl.DeviceIdType.MESH

POOL, FLIP, LOCAL, MATE, PEER, FILLED, LINK, PICK = range(8)
SOURCES = ((0, True, True), (1, True, True), (1, False, False), (2, True, True), (2, False, False),
           (3, True, True), (3, False, False), (4, True, False))


def kernel(tab, x_hbm, prec, out, pool, stage, stk, wt, yt, vv, tile, oc, ub, uf, sb, own, yb, yr, uc, ms, mx, mz, mloc,
           wc, wg, og, loc_sem, zs_sem, zr_sem, xs_sem, xr_sem, bs_sem, br_sem, ys_sem, yr_sem, as_sem, ar_sem,
           ms_sem, mr_sem, gs_sem, gr_sem, hs_sem, hr_sem):
    samp, feat = lax.axis_index("samp"), lax.axis_index("feat")
    y, c = samp // NC, samp % NC
    x, z = feat // NZ, feat % NZ

    def at_x(d):
        return (x + d) % NX

    def at_z(d):
        return (z + d) % NZ

    def at_y(d):
        return (y + d) % NY

    def dev(yy, cc, xx, zz):
        return (yy * NC + cc, xx * NZ + zz)

    def remote(src, dst, ssem, rsem, device):
        return pltpu.make_async_remote_copy(src_ref=src, dst_ref=dst, send_sem=ssem, recv_sem=rsem, device_id=device,
                                            device_id_type=MESH)

    barrier = pltpu.get_barrier_semaphore()
    peers = ([dev(y, c, at_x(d), z) for d in range(1, NX)] + [dev(y, c, x, at_z(d)) for d in range(1, NZ)]
             + [dev(at_y(d), c, x, z) for d in range(1, NY)] + [dev(y, 1 - c, x, z)])
    loads = [pltpu.make_async_copy(x_hbm.at[:, pl.ds(r * BK, BK)], pool.at[z * BR + r], loc_sem.at[r]) for r in range(BR)]
    for load in loads:
        load.start()
    for peer in peers:
        pl.semaphore_signal(barrier, inc=1, device_id=peer, device_id_type=MESH)
    pl.semaphore_wait(barrier, len(peers))

    def z_copy(up, t, r):
        source = at_z(NZ - t) if up else at_z(t)
        slot = source * BR + r
        side = 0 if up else 1
        return remote(pool.at[slot], pool.at[slot], zs_sem.at[side, t, r], zr_sem.at[side, t, r],
                      dev(y, c, x, at_z(1) if up else at_z(NZ - 1)))

    def z_rows(up, t):
        if t < 3:
            return range(BR)
        return range(0, BR // 2) if up else range(BR // 2, BR)

    def x_copy(q, kind):
        t, up, _ = SOURCES[q]
        zsrc = at_z(NZ - t) if up else at_z(t)
        upward = SOURCES[q][2]
        ahead = 1 if upward else NX - 1
        if kind == 0:
            src, dst, to = stage.at[q, 0], pool.at[NF + x * NZ + zsrc], at_x(1)
        elif kind == 1:
            src, dst, to = stage.at[q, 1], pool.at[NF + x * NZ + zsrc], at_x(NX - 1)
        elif kind == 2:
            src, dst, to = stage.at[q, 2], pool.at[NF + at_x(ahead) * NZ + zsrc], at_x(ahead)
        else:
            src, dst, to = pool.at[NF + x * NZ + zsrc], pool.at[NF + at_x(NX - ahead) * NZ + zsrc], at_x(ahead)
        return remote(src, dst, xs_sem.at[q, kind], xr_sem.at[q, kind], dev(y, c, to, z))

    def pick(q):
        t, up, _ = SOURCES[q]
        zsrc = at_z(NZ - t) if up else at_z(t)
        rows = ROWS // 4
        for kind, d in ((2, 2), (0, 1), (1, NX - 1)):
            chosen = tab[PICK, zsrc * NX + at_x(d)]

            def part(i, carry):
                at = pl.ds(pl.multiple_of(i * rows, rows), rows)
                got = pool[zsrc * BR, at, :]
                for r in range(1, BR):
                    got = jnp.where(chosen == r, pool[zsrc * BR + r, at, :], got)
                stage[q, kind, at, :] = got
                return carry

            lax.fori_loop(0, 4, part, 0)
            x_copy(q, kind).start()

    def relay(q):
        x_copy(q, 2).wait_recv()
        x_copy(q, 3).start()

    for r, load in enumerate(loads):
        load.wait()
        z_copy(True, 0, r).start()
        z_copy(False, 0, r).start()
    pick(0)

    def first(b, carry):
        block = jnp.where(tab[FILLED, b] > 0, prec[b], 0.0)
        turned = block.T
        wt[b] = turned.astype(BF16)
        tile[...] = jnp.where(tab[FLIP, b] > 0, turned, block)
        oc[b] = tile[pl.ds(pl.multiple_of(samp * CH, CH), CH), :]
        return carry

    lax.fori_loop(0, NBK, first, 0)

    for t in range(1, 5):
        for r in range(BR):
            for up in (True, False):
                if r in z_rows(up, t - 1):
                    z_copy(up, t - 1, r).wait_recv()
                    if t < 4 and r in z_rows(up, t):
                        z_copy(up, t, r).start()
        for q in range(len(SOURCES)):
            if SOURCES[q][0] == t:
                pick(q)
        for q in range(len(SOURCES)):
            if SOURCES[q][0] == t - 1:
                relay(q)
    relay(len(SOURCES) - 1)
    for q in range(len(SOURCES)):
        for kind in (0, 1, 3):
            x_copy(q, kind).wait_recv()
    for up in (True, False):
        for t in range(4):
            for r in z_rows(up, t):
                z_copy(up, t, r).wait_send()
    for q in range(len(SOURCES)):
        for kind in range(4):
            x_copy(q, kind).wait_send()

    def gather_slots(b, carry):
        j, k = b // SL, b % SL
        stk[j, :, pl.ds(pl.multiple_of(k * BK, BK), BK)] = pool[tab[POOL, b]]
        return carry

    lax.fori_loop(0, NBK, gather_slots, 0)

    def pair_copy(it, j):
        return remote(ub.at[it, j], sb.at[it, j], bs_sem.at[it, j], br_sem.at[it, j], dev(y, 1 - c, x, z))

    def y_copy(it, j, d):
        return remote(yb.at[it, j, d - 1], yr.at[it, j, d - 1], ys_sem.at[it, j, d - 1], yr_sem.at[it, j, d - 1],
                      dev(at_y(d), c, x, z))

    def pass_on(it, j):
        pair_copy(it, j).wait_recv()
        for d in range(NY):
            yy = at_y(d)
            summed = uf[j, yy] + sb[it, j, yy].astype(F32)
            if d == 0:
                own[j] = summed
            else:
                yb[it, j, d - 1] = summed.astype(BF16)
                y_copy(it, j, d).start()

    def mx_copy(it, d):
        return remote(ms.at[it, at_x(d)], mx.at[it, x], as_sem.at[it, d - 1], ar_sem.at[it, d - 1], dev(y, c, at_x(d), z))

    def mz_copy(it, d):
        return remote(mx.at[it, :, at_z(d)], mz.at[it, z], ms_sem.at[it, d - 1], mr_sem.at[it, d - 1],
                      dev(y, c, x, at_z(d)))

    def gather_y(src, dst, it, d):
        return remote(src, dst.at[samp], gs_sem.at[it, d - 1], gr_sem.at[it, d - 1], dev(at_y(d), c, x, z))

    def gather_c(src, dst, it, d):
        holder = at_y(NY - d) * NC + c if d else samp
        return remote(src if d == 0 else dst.at[holder], dst.at[holder], hs_sem.at[it, d], hr_sem.at[it, d],
                      dev(y, 1 - c, x, z))

    def gather_samp(src, dst, it):
        for d in range(1, NY):
            gather_y(src, dst, it, d).start()
        gather_c(src, dst, it, 0).start()
        dst[samp] = src[...]
        for d in range(1, NY):
            gather_y(src, dst, it, d).wait_recv()
            gather_c(src, dst, it, d).start()
        for d in range(NY):
            gather_c(src, dst, it, d).wait_recv()

    def gather_sent(src, dst, it):
        for d in range(1, NY):
            gather_y(src, dst, it, d).wait_send()
        for d in range(NY):
            gather_c(src, dst, it, d).wait_send()

    def iteration(it, carry):
        def row(j, carry):
            part = ROWS // 4
            weights = wt[pl.ds(pl.multiple_of(j * SL, SL), SL)].reshape(SL * BK, BK)
            for i in range(4):
                projected = jnp.dot(stk[j, i * part:(i + 1) * part, :], weights, preferred_element_type=F32)
                yt[:, i * part:(i + 1) * part] = projected.astype(BF16).T
            vv[...] = jnp.dot(yt[...], stk[j], preferred_element_type=F32)
            for k in range(SL):
                block = vv[:, k * BK:(k + 1) * BK]
                turned = block.T
                if k == 0:
                    block = 0.5 * (block + turned)
                else:
                    block = jnp.where(tab[FLIP, j * SL + k] > 0, turned, block)
                cut = block.reshape(NY, NC, CH, BK)
                even, odd = cut[:, 0], cut[:, 1]
                uf[j, :, k] = jnp.where(c == 0, even, odd)
                ub[it, j, :, k] = jnp.where(c == 0, odd, even).astype(BF16)
            pair_copy(it, j).start()

            @pl.when(j > 0)
            def _():
                pass_on(it, j - 1)

            return carry

        lax.fori_loop(0, BR, row, 0)
        pass_on(it, BR - 1)

        def finish(j, carry):
            total = own[j]
            for d in range(1, NY):
                y_copy(it, j, d).wait_recv()
                total = total + yr[it, j, d - 1].astype(F32)
            uc[pl.ds(pl.multiple_of(j * SL, SL), SL)] = total
            return carry

        lax.fori_loop(0, BR, finish, 0)

        def post(p, carry):
            ms[it, p // NZ, p % NZ] = uc[tab[LINK, p]].astype(BF16)
            return carry

        lax.fori_loop(0, NF, post, 0)
        for d in range(1, NX):
            mx_copy(it, d).start()
        mx[it, x] = ms[it, x]
        for d in range(1, NX):
            mx_copy(it, d).wait_recv()
        for d in range(1, NZ):
            mz_copy(it, d).start()
        mloc[z] = mx[it, :, z]
        for d in range(1, NZ):
            mz_copy(it, d).wait_recv()
            source = at_z(NZ - d)
            mloc[source] = mz[it, source]

        def update(j, carry):
            for k in range(SL):
                b = j * SL + k
                gradient = uc[b]
                if k > 0:
                    peer = tab[PEER, b]
                    mirrored = jnp.where(tab[LOCAL, b] > 0, uc[tab[MATE, b]], mloc[peer // NX, peer % NX].astype(F32))
                    gradient = 0.5 * (gradient + mirrored)
                stepped = oc[b] - STEP * (gradient * (1.0 / (ROWS * NS)))
                result = jnp.where(stepped > 0, jnp.maximum(stepped - SHRINK, 0.0), jnp.minimum(stepped + SHRINK, 0.0))
                if k == 0:
                    rooted = 0.5 * (stepped + jnp.sqrt(stepped * stepped + 4.0 * STEP))
                    across = lax.broadcasted_iota(jnp.int32, (CH, BK), 1)
                    down = lax.broadcasted_iota(jnp.int32, (CH, BK), 0) + samp * CH
                    result = jnp.where(across == down, rooted, result)
                result = jnp.where(tab[FILLED, b] > 0, result, 0.0)
                oc[b] = result
                wc[it, b] = result.astype(BF16)
            return carry

        lax.fori_loop(0, BR, update, 0)

        @pl.when(it < ITERS - 1)
        def _():
            gather_samp(wc.at[it], wg.at[it], it)

            def turn(b, carry):
                block = wg[it, :, b].reshape(BK, BK)
                wt[b] = jnp.where(tab[FLIP, b] > 0, block, block.T)
                return carry

            lax.fori_loop(0, NBK, turn, 0)

        return carry

    lax.fori_loop(0, ITERS, iteration, 0)
    gather_samp(oc, og, ITERS - 1)

    def store(b, carry):
        block = og[:, b].reshape(BK, BK)
        out[b] = jnp.where(tab[FLIP, b] > 0, block.T, block)
        return carry

    lax.fori_loop(0, NBK, store, 0)

    def sent(it, carry):
        for j in range(BR):
            pair_copy(it, j).wait_send()
            for d in range(1, NY):
                y_copy(it, j, d).wait_send()
        for d in range(1, NX):
            mx_copy(it, d).wait_send()
        for d in range(1, NZ):
            mz_copy(it, d).wait_send()

        @pl.when(it < ITERS - 1)
        def _():
            gather_sent(wc.at[it], wg.at[it], it)

        return carry

    lax.fori_loop(0, ITERS, sent, 0)
    gather_sent(oc, og, ITERS - 1)


def tables(col_blocks):
    feat = lax.axis_index("feat")
    cols = col_blocks.reshape(NBK)
    filled = cols >= 0
    place = jnp.arange(NBK, dtype=jnp.int32)
    row_ids = feat * BR + place // SL
    holder = jnp.where(filled, cols // BR, feat)
    inside = jnp.where(filled, cols % BR, 0)
    hx, hz = holder // NZ, holder % NZ
    same_x = hx == feat // NZ
    pool = jnp.where(same_x, hz * BR + inside, NF + holder)
    flip = filled & (cols < row_ids)
    local = filled & (holder == feat)
    pair = (cols[:, None] == row_ids[None, :]) & (cols[None, :] == row_ids[:, None])
    mate = jnp.sum(jnp.where(pair, place[None, :], 0), axis=1)
    linked = (filled & (holder != feat))[None, :] & (holder[None, :] == jnp.arange(NF, dtype=jnp.int32)[:, None])
    link = jnp.sum(jnp.where(linked, place[None, :], 0), axis=1)
    rows = jnp.sum(jnp.where(linked, inside[None, :], 0), axis=1)
    groups = [[xx * NZ + zz for xx in range(NX)] for zz in range(NZ)]
    near = lax.all_gather(rows, "feat", axis_index_groups=groups).reshape(NX, NX, NZ)
    picks = lax.dynamic_index_in_dim(near, feat // NZ, axis=1, keepdims=False).T.reshape(NF)
    return jnp.stack([pool, flip.astype(jnp.int32), local.astype(jnp.int32), mate, hz * NX + hx, filled.astype(jnp.int32),
                      link, picks]).astype(jnp.int32)


def local(samples, precision, col_blocks):
    vmem = pl.BlockSpec(memory_space=pltpu.VMEM)
    piece = (SL, CH, BK)
    dma = pltpu.SemaphoreType.DMA
    result = pl.pallas_call(
        kernel,
        out_shape=jax.ShapeDtypeStruct((NBK, BK, BK), F32),
        in_specs=[pl.BlockSpec(memory_space=pltpu.SMEM), pl.BlockSpec(memory_space=pl.ANY), vmem],
        out_specs=vmem,
        scratch_shapes=[
            pltpu.VMEM((2 * NF, ROWS, BK), BF16),
            pltpu.VMEM((NZ, 3, ROWS, BK), BF16),
            pltpu.VMEM((BR, ROWS, SL * BK), BF16),
            pltpu.VMEM((NBK, BK, BK), BF16),
            pltpu.VMEM((BK, ROWS), BF16),
            pltpu.VMEM((BK, SL * BK), F32),
            pltpu.VMEM((BK, BK), F32),
            pltpu.VMEM((NBK, CH, BK), F32),
            pltpu.VMEM((ITERS, BR, NY) + piece, BF16),
            pltpu.VMEM((BR, NY) + piece, F32),
            pltpu.VMEM((ITERS, BR, NY) + piece, BF16),
            pltpu.VMEM((BR,) + piece, F32),
            pltpu.VMEM((ITERS, BR, NY - 1) + piece, BF16),
            pltpu.VMEM((ITERS, BR, NY - 1) + piece, BF16),
            pltpu.VMEM((NBK, CH, BK), F32),
            pltpu.VMEM((ITERS, NX, NZ, CH, BK), BF16),
            pltpu.VMEM((ITERS, NX, NZ, CH, BK), BF16),
            pltpu.VMEM((ITERS, NZ, NX, CH, BK), BF16),
            pltpu.VMEM((NZ, NX, CH, BK), BF16),
            pltpu.VMEM((ITERS, NBK, CH, BK), BF16),
            pltpu.VMEM((ITERS - 1, NS, NBK, CH, BK), BF16),
            pltpu.VMEM((NS, NBK, CH, BK), F32),
            dma((BR,)),
            dma((2, 4, BR)), dma((2, 4, BR)),
            dma((NZ, 4)), dma((NZ, 4)),
            dma((ITERS, BR)), dma((ITERS, BR)),
            dma((ITERS, BR, NY - 1)), dma((ITERS, BR, NY - 1)),
            dma((ITERS, NX - 1)), dma((ITERS, NX - 1)),
            dma((ITERS, NZ - 1)), dma((ITERS, NZ - 1)),
            dma((ITERS, NY - 1)), dma((ITERS, NY - 1)),
            dma((ITERS, NY)), dma((ITERS, NY)),
        ],
        compiler_params=pltpu.CompilerParams(collective_id=0, has_side_effects=True, vmem_limit_bytes=60 * 2**20),
        name="prox_iterations",
    )(tables(col_blocks), samples, precision.reshape(NBK, BK, BK))
    return result.reshape(BR, SL, BK, BK)


def solution(mesh):
    if mesh.shape["samp"] != NS or mesh.shape["feat"] != NF:
        raise ValueError("unexpected mesh")
    return jax.shard_map(
        local,
        mesh=mesh,
        in_specs=(P("samp", "feat"), P("feat", None, None, None), P("feat", None)),
        out_specs=P("feat", None, None, None),
        check_vma=False,
    )
```

```python
import functools

import jax
import jax.numpy as jnp
from jax import lax
from jax.experimental import pallas as pl
from jax.experimental.pallas import tpu as pltpu
from jax.sharding import PartitionSpec as P

ITERS = 3
STEP = 0.2
SHRINK = 0.2 * 0.25
NX, NZ, NY, NC = 4, 8, 4, 2
NS = NY * NC
NF = NX * NZ
BR, SL, BK = 4, 8, 128
NBK = BR * SL
CH = BK // NS
ROWS = 1024
F32, BF16 = jnp.float32, jnp.bfloat16
MESH = pl.DeviceIdType.MESH

HALF = ROWS // 2

POOL, FLIP, LOCAL, MATE, PEER, FILLED, LINK, PICK = range(8)
SOURCES = ((0, True), (1, True), (1, False), (2, True), (2, False), (3, True), (3, False), (4, True))


def kernel(tab, x_hbm, prec_hbm, out_hbm, pool, stage, stk, wt, yt, vv, tile, prec, oc,
           ub, uf, sb, own, yb, yr, uc, ms, mz, mloc, wc, wg, og, result_rows, loc_sem, out_sem,
           zs_sem, zr_sem, xs_sem, xr_sem, bs_sem, br_sem, ys_sem, yr_sem, ms_sem, mr_sem, gs_sem, gr_sem,
           hs_sem, hr_sem):
    samp, feat = lax.axis_index("samp"), lax.axis_index("feat")
    y, c = samp // NC, samp % NC
    x, z = feat // NZ, feat % NZ

    def at_x(d):
        return (x + d) % NX

    def at_z(d):
        return (z + d) % NZ

    def at_y(d):
        return (y + d) % NY

    def dev(yy, cc, xx, zz):
        return (yy * NC + cc, xx * NZ + zz)

    def remote(src, dst, ssem, rsem, device):
        return pltpu.make_async_remote_copy(src_ref=src, dst_ref=dst, send_sem=ssem, recv_sem=rsem, device_id=device,
                                            device_id_type=MESH)

    barrier = pltpu.get_barrier_semaphore()
    peers = ([dev(y, c, at_x(i // NZ), at_z(i % NZ)) for i in range(1, NF)]
             + [dev(at_y(d), c, x, z) for d in range(1, NY)] + [dev(y, 1 - c, x, z)])
    for peer in peers:
        pl.semaphore_signal(barrier, inc=1, device_id=peer, device_id_type=MESH)
    loads = [pltpu.make_async_copy(x_hbm.at[:, pl.ds(r * BK, BK)], pool.at[z * BR + r], loc_sem.at[r]) for r in range(BR)]
    loads.append(pltpu.make_async_copy(prec_hbm, prec, loc_sem.at[BR]))
    for load in loads:
        load.start()
    pl.semaphore_wait(barrier, len(peers))

    def z_copy(up, t, h, r):
        source = at_z(NZ - t) if up else at_z(t)
        piece = pool.at[source * BR + r, pl.ds(h * HALF, HALF)]
        side = 0 if up else 1
        return remote(piece, piece, zs_sem.at[side, t, h, r], zr_sem.at[side, t, h, r],
                      dev(y, c, x, at_z(1) if up else at_z(NZ - 1)))

    def z_halves(up, t):
        if t < 3:
            return (0, 1)
        return (0,) if up else (1,)

    def x_copy(q, h, e):
        t, up = SOURCES[q]
        zsrc = at_z(NZ - t) if up else at_z(t)
        rows = pl.ds(h * HALF, HALF)
        return remote(stage.at[q, e - 1, rows], pool.at[NF + x * NZ + zsrc, rows], xs_sem.at[q, h, e - 1],
                      xr_sem.at[q, h, e - 1], dev(y, c, at_x(e), z))

    def pick(q, h):
        t, up = SOURCES[q]
        zsrc = at_z(NZ - t) if up else at_z(t)
        rows = HALF // 2
        for e in (2, 1, 3):
            chosen = tab[PICK, zsrc * NX + at_x(e)]

            def part(i, carry):
                at = pl.ds(pl.multiple_of(h * HALF + i * rows, rows), rows)
                got = pool[zsrc * BR, at, :]
                for r in range(1, BR):
                    got = jnp.where(chosen == r, pool[zsrc * BR + r, at, :], got)
                stage[q, e - 1, at, :] = got
                return carry

            lax.fori_loop(0, 2, part, 0)
            x_copy(q, h, e).start()

    for r in range(BR):
        loads[r].wait()
    for h in range(2):
        for r in range(BR):
            z_copy(True, 0, h, r).start()
            z_copy(False, 0, h, r).start()
    for h in range(2):
        pick(0, h)

    def first(b, carry):
        block = jnp.where(tab[FILLED, b] > 0, prec[b], 0.0)
        turned = block.T
        wt[b] = turned.astype(BF16)
        tile[...] = jnp.where(tab[FLIP, b] > 0, turned, block)
        oc[b] = tile[pl.ds(pl.multiple_of(samp * CH, CH), CH), :]
        return carry

    for t in range(1, 5):
        for h in range(2):
            for r in range(BR):
                for up in (True, False):
                    if h in z_halves(up, t - 1):
                        z_copy(up, t - 1, h, r).wait_recv()
                        if t < 4 and h in z_halves(up, t):
                            z_copy(up, t, h, r).start()
            for q in range(len(SOURCES)):
                if SOURCES[q][0] == t:
                    pick(q, h)
            if t == 1 and h == 0:
                loads[BR].wait()
                lax.fori_loop(0, NBK, first, 0)
    for q in range(len(SOURCES)):
        for h in range(2):
            for e in range(1, NX):
                x_copy(q, h, e).wait_recv()
    for up in (True, False):
        for t in range(4):
            for h in z_halves(up, t):
                for r in range(BR):
                    z_copy(up, t, h, r).wait_send()
    for q in range(len(SOURCES)):
        for h in range(2):
            for e in range(1, NX):
                x_copy(q, h, e).wait_send()

    def gather_slots(b, carry):
        j, k = b // SL, b % SL
        stk[j, :, pl.ds(pl.multiple_of(k * BK, BK), BK)] = pool[tab[POOL, b]]
        return carry

    lax.fori_loop(0, NBK, gather_slots, 0)

    last = ITERS - 1

    def pair_copy(it, j):
        return remote(ub.at[it, j], sb.at[it, j], bs_sem.at[it, j], br_sem.at[it, j], dev(y, 1 - c, x, z))

    def y_copy(it, j, d):
        return remote(yb.at[it, j, d - 1], yr.at[it, j, d - 1], ys_sem.at[it, j, d - 1], yr_sem.at[it, j, d - 1],
                      dev(at_y(d), c, x, z))

    def pass_on(it, j):
        pair_copy(it, j).wait_recv()
        for d in (2, 1, 3, 0):
            yy = at_y(d)
            summed = uf[j, yy] + sb[it, j, yy].astype(F32)
            if d == 0:
                own[j] = summed
            else:
                yb[it, j, d - 1] = summed.astype(BF16)
                y_copy(it, j, d).start()

    def mirror_copy(it, i):
        e, d = i // NZ, i % NZ
        return remote(ms.at[it, i], mz.at[it, i], ms_sem.at[it, i], mr_sem.at[it, i], dev(y, c, at_x(e), at_z(d)))

    def piece_of(ref, j):
        return ref.at[pl.ds(pl.multiple_of(j * SL, SL), SL)]

    def gather_y(src, dst, it, j, d):
        return remote(piece_of(src, j), dst.at[j, samp], gs_sem.at[it, j, d - 1], gr_sem.at[it, j, d - 1],
                      dev(at_y(d), c, x, z))

    def gather_c(src, dst, it, j, e):
        holder = at_y(NY - e) * NC + c if e else samp
        source = dst.at[j, holder] if e else piece_of(src, j)
        return remote(source, dst.at[j, holder], hs_sem.at[it, j, e], hr_sem.at[it, j, e], dev(y, 1 - c, x, z))

    def gather_start(src, dst, it, j):
        for d in (2, 1, 3):
            gather_y(src, dst, it, j, d).start()
        gather_c(src, dst, it, j, 0).start()
        dst[j, samp] = src[pl.ds(pl.multiple_of(j * SL, SL), SL)]

    def gather_turn(src, dst, it, j):
        for d in (1, 3, 2):
            gather_y(src, dst, it, j, d).wait_recv()
            gather_c(src, dst, it, j, d).start()

    def gather_done(src, dst, it, j):
        for e in range(NY):
            gather_c(src, dst, it, j, e).wait_recv()

    def gather_sent(src, dst, it):
        def sent(j, carry):
            for d in range(1, NY):
                gather_y(src, dst, it, j, d).wait_send()
            for e in range(NY):
                gather_c(src, dst, it, j, e).wait_send()
            return carry

        lax.fori_loop(0, BR, sent, 0)

    def iteration(it, carry):
        @pl.when(it > 0)
        def _():
            gather_turn(wc.at[it - 1], wg.at[it - 1], it - 1, 0)

        def row(j, carry):
            @pl.when(it > 0)
            def _():
                gather_done(wc.at[it - 1], wg.at[it - 1], it - 1, j)
                for k in range(SL):
                    block = wg[it - 1, j, :, k].reshape(BK, BK)
                    wt[j * SL + k] = jnp.where(tab[FLIP, j * SL + k] > 0, block, block.T)

            part = ROWS // 4
            weights = wt[pl.ds(pl.multiple_of(j * SL, SL), SL)].reshape(SL * BK, BK)
            for i in range(4):
                projected = jnp.dot(stk[j, i * part:(i + 1) * part, :], weights, preferred_element_type=F32)
                yt[:, i * part:(i + 1) * part] = projected.astype(BF16).T
            vv[...] = jnp.dot(yt[...], stk[j], preferred_element_type=F32)

            @pl.when((it > 0) & (j < BR - 1))
            def _():
                gather_turn(wc.at[it - 1], wg.at[it - 1], it - 1, j + 1)

            for k in range(SL):
                block = vv[:, k * BK:(k + 1) * BK]
                turned = block.T
                if k == 0:
                    block = 0.5 * (block + turned)
                else:
                    block = jnp.where(tab[FLIP, j * SL + k] > 0, turned, block)
                cut = block.reshape(NY, NC, CH, BK)
                even, odd = cut[:, 0], cut[:, 1]
                uf[j, :, k] = jnp.where(c == 0, even, odd)
                ub[it, j, :, k] = jnp.where(c == 0, odd, even).astype(BF16)
            pair_copy(it, j).start()

            @pl.when(j > 0)
            def _():
                pass_on(it, j - 1)

            return carry

        lax.fori_loop(0, BR, row, 0)
        pass_on(it, BR - 1)

        def finish(j, carry):
            total = own[j]
            for d in range(1, NY):
                y_copy(it, j, d).wait_recv()
                total = total + yr[it, j, d - 1].astype(F32)
            uc[pl.ds(pl.multiple_of(j * SL, SL), SL)] = total
            return carry

        lax.fori_loop(0, BR, finish, 0)

        def post(i, carry):
            ms[it, i] = uc[tab[LINK, at_x(i // NZ) * NZ + at_z(i % NZ)]].astype(BF16)
            mirror_copy(it, i).start()
            return carry

        lax.fori_loop(1, NF, post, 0)

        def collect(i, carry):
            mirror_copy(it, i).wait_recv()
            mloc[at_z(NZ - i % NZ), at_x(NX - i // NZ)] = mz[it, i]
            return carry

        lax.fori_loop(1, NF, collect, 0)

        def update(j, carry):
            for k in range(SL):
                b = j * SL + k
                gradient = uc[b]
                if k > 0:
                    peer = tab[PEER, b]
                    mirrored = jnp.where(tab[LOCAL, b] > 0, uc[tab[MATE, b]], mloc[peer // NX, peer % NX].astype(F32))
                    gradient = 0.5 * (gradient + mirrored)
                stepped = oc[b] - STEP * (gradient * (1.0 / (ROWS * NS)))
                result = jnp.where(stepped > 0, jnp.maximum(stepped - SHRINK, 0.0), jnp.minimum(stepped + SHRINK, 0.0))
                if k == 0:
                    rooted = 0.5 * (stepped + jnp.sqrt(stepped * stepped + 4.0 * STEP))
                    across = lax.broadcasted_iota(jnp.int32, (CH, BK), 1)
                    down = lax.broadcasted_iota(jnp.int32, (CH, BK), 0) + samp * CH
                    result = jnp.where(across == down, rooted, result)
                result = jnp.where(tab[FILLED, b] > 0, result, 0.0)
                oc[b] = result
                wc[it, b] = result.astype(BF16)

            @pl.when(it < last)
            def _():
                gather_start(wc.at[it], wg.at[it], it, j)

            @pl.when(it == last)
            def _():
                gather_start(oc, og, last, j)

            return carry

        lax.fori_loop(0, BR, update, 0)
        return carry

    lax.fori_loop(0, ITERS, iteration, 0)

    def out_copy(j):
        rows = pl.ds(pl.multiple_of(j * SL, SL), SL)
        return pltpu.make_async_copy(result_rows.at[rows], out_hbm.at[rows], out_sem.at[j])

    gather_turn(oc, og, last, 0)

    def store(j, carry):
        gather_done(oc, og, last, j)
        for k in range(SL):
            block = og[j, :, k].reshape(BK, BK)
            result_rows[j * SL + k] = jnp.where(tab[FLIP, j * SL + k] > 0, block.T, block)
        out_copy(j).start()

        @pl.when(j < BR - 1)
        def _():
            gather_turn(oc, og, last, j + 1)

        return carry

    lax.fori_loop(0, BR, store, 0)

    def sent(it, carry):
        for j in range(BR):
            pair_copy(it, j).wait_send()
            for d in range(1, NY):
                y_copy(it, j, d).wait_send()

        def mirror_sent(i, carry):
            mirror_copy(it, i).wait_send()
            return carry

        lax.fori_loop(1, NF, mirror_sent, 0)

        @pl.when(it < last)
        def _():
            gather_sent(wc.at[it], wg.at[it], it)

        return carry

    lax.fori_loop(0, ITERS, sent, 0)
    gather_sent(oc, og, last)
    for j in range(BR):
        out_copy(j).wait()


def tables(col_blocks):
    feat = lax.axis_index("feat")
    cols = col_blocks.reshape(NBK)
    filled = cols >= 0
    place = jnp.arange(NBK, dtype=jnp.int32)
    row_ids = feat * BR + place // SL
    holder = jnp.where(filled, cols // BR, feat)
    inside = jnp.where(filled, cols % BR, 0)
    hx, hz = holder // NZ, holder % NZ
    same_x = hx == feat // NZ
    pool = jnp.where(same_x, hz * BR + inside, NF + holder)
    flip = filled & (cols < row_ids)
    local = filled & (holder == feat)
    pair = (cols[:, None] == row_ids[None, :]) & (cols[None, :] == row_ids[:, None])
    mate = jnp.sum(jnp.where(pair, place[None, :], 0), axis=1)
    linked = (filled & (holder != feat))[None, :] & (holder[None, :] == jnp.arange(NF, dtype=jnp.int32)[:, None])
    link = jnp.sum(jnp.where(linked, place[None, :], 0), axis=1)
    rows = jnp.sum(jnp.where(linked, inside[None, :], 0), axis=1)
    groups = [[xx * NZ + zz for xx in range(NX)] for zz in range(NZ)]
    near = lax.all_gather(rows, "feat", axis_index_groups=groups).reshape(NX, NX, NZ)
    picks = lax.dynamic_index_in_dim(near, feat // NZ, axis=1, keepdims=False).T.reshape(NF)
    return jnp.stack([pool, flip.astype(jnp.int32), local.astype(jnp.int32), mate, hz * NX + hx, filled.astype(jnp.int32),
                      link, picks]).astype(jnp.int32)


def local(samples, precision, col_blocks):
    anywhere = pl.BlockSpec(memory_space=pl.ANY)
    piece = (SL, CH, BK)
    dma = pltpu.SemaphoreType.DMA
    result = pl.pallas_call(
        kernel,
        out_shape=jax.ShapeDtypeStruct((NBK, BK, BK), F32),
        in_specs=[pl.BlockSpec(memory_space=pltpu.SMEM), anywhere, anywhere],
        out_specs=anywhere,
        scratch_shapes=[
            pltpu.VMEM((2 * NF, ROWS, BK), BF16),
            pltpu.VMEM((NZ, 3, ROWS, BK), BF16),
            pltpu.VMEM((BR, ROWS, SL * BK), BF16),
            pltpu.VMEM((NBK, BK, BK), BF16),
            pltpu.VMEM((BK, ROWS), BF16),
            pltpu.VMEM((BK, SL * BK), F32),
            pltpu.VMEM((BK, BK), F32),
            pltpu.VMEM((NBK, BK, BK), F32),
            pltpu.VMEM((NBK, CH, BK), F32),
            pltpu.VMEM((ITERS, BR, NY) + piece, BF16),
            pltpu.VMEM((BR, NY) + piece, F32),
            pltpu.VMEM((ITERS, BR, NY) + piece, BF16),
            pltpu.VMEM((BR,) + piece, F32),
            pltpu.VMEM((ITERS, BR, NY - 1) + piece, BF16),
            pltpu.VMEM((ITERS, BR, NY - 1) + piece, BF16),
            pltpu.VMEM((NBK, CH, BK), F32),
            pltpu.VMEM((ITERS, NF, CH, BK), BF16),
            pltpu.VMEM((ITERS, NF, CH, BK), BF16),
            pltpu.VMEM((NZ, NX, CH, BK), BF16),
            pltpu.VMEM((ITERS, NBK, CH, BK), BF16),
            pltpu.VMEM((ITERS - 1, BR, NS) + piece, BF16),
            pltpu.VMEM((BR, NS) + piece, F32),
            pltpu.VMEM((NBK, BK, BK), F32),
            dma((BR + 1,)), dma((BR,)),
            dma((2, 4, 2, BR)), dma((2, 4, 2, BR)),
            dma((NZ, 2, NX - 1)), dma((NZ, 2, NX - 1)),
            dma((ITERS, BR)), dma((ITERS, BR)),
            dma((ITERS, BR, NY - 1)), dma((ITERS, BR, NY - 1)),
            dma((ITERS, NF)), dma((ITERS, NF)),
            dma((ITERS, BR, NY - 1)), dma((ITERS, BR, NY - 1)),
            dma((ITERS, BR, NY)), dma((ITERS, BR, NY)),
        ],
        compiler_params=pltpu.CompilerParams(collective_id=0, has_side_effects=True, vmem_limit_bytes=60 * 2**20),
        name="prox_iterations",
    )(tables(col_blocks), samples, precision.reshape(NBK, BK, BK))
    return result.reshape(BR, SL, BK, BK)


def solution(mesh):
    if mesh.shape["samp"] != NS or mesh.shape["feat"] != NF:
        raise ValueError("unexpected mesh")
    return jax.shard_map(
        local,
        mesh=mesh,
        in_specs=(P("samp", "feat"), P("feat", None, None, None), P("feat", None)),
        out_specs=P("feat", None, None, None),
        check_vma=False,
    )
```

```python
import functools

import jax
import jax.numpy as jnp
from jax import lax
from jax.experimental import pallas as pl
from jax.experimental.pallas import tpu as pltpu
from jax.sharding import PartitionSpec as P

ITERS = 3
STEP = 0.2
SHRINK = 0.2 * 0.25
NX, NZ, NY, NC = 4, 8, 4, 2
NS = NY * NC
NF = NX * NZ
BR, SL, BK = 4, 8, 128
NBK = BR * SL
CH = BK // NS
ROWS = 1024
F32, BF16 = jnp.float32, jnp.bfloat16
MESH = pl.DeviceIdType.MESH

HALF = ROWS // 2

POOL, FLIP, LOCAL, MATE, PEER, FILLED, LINK, PICK = range(8)
SOURCES = ((0, True), (1, True), (1, False), (2, True), (2, False), (3, True), (3, False), (4, True))


def kernel(tab, x_hbm, prec_hbm, out_hbm, pool, stage, stk, wt, yt, vv, tile, prec, oc,
           ub, uf, sb, own, yb, yr, uc, ms, mz, mloc, wc, wg, og, result_rows, loc_sem, out_sem,
           zs_sem, zr_sem, xs_sem, xr_sem, bs_sem, br_sem, ys_sem, yr_sem, ms_sem, mr_sem, gs_sem, gr_sem,
           hs_sem, hr_sem):
    samp, feat = lax.axis_index("samp"), lax.axis_index("feat")
    y, c = samp // NC, samp % NC
    x, z = feat // NZ, feat % NZ

    def at_x(d):
        return (x + d) % NX

    def at_z(d):
        return (z + d) % NZ

    def at_y(d):
        return (y + d) % NY

    def dev(yy, cc, xx, zz):
        return (yy * NC + cc, xx * NZ + zz)

    def remote(src, dst, ssem, rsem, device):
        return pltpu.make_async_remote_copy(src_ref=src, dst_ref=dst, send_sem=ssem, recv_sem=rsem, device_id=device,
                                            device_id_type=MESH)

    barrier = pltpu.get_barrier_semaphore()
    peers = ([dev(y, c, at_x(i // NZ), at_z(i % NZ)) for i in range(1, NF)]
             + [dev(at_y(d), c, x, z) for d in range(1, NY)] + [dev(y, 1 - c, x, z)])
    for peer in peers:
        pl.semaphore_signal(barrier, inc=1, device_id=peer, device_id_type=MESH)
    loads = [pltpu.make_async_copy(x_hbm.at[:, pl.ds(r * BK, BK)], pool.at[z * BR + r], loc_sem.at[r]) for r in range(BR)]
    loads.append(pltpu.make_async_copy(prec_hbm, prec, loc_sem.at[BR]))
    for load in loads:
        load.start()
    pl.semaphore_wait(barrier, len(peers))

    def z_copy(up, t, h, r):
        source = at_z(NZ - t) if up else at_z(t)
        piece = pool.at[source * BR + r, pl.ds(h * HALF, HALF)]
        side = 0 if up else 1
        return remote(piece, piece, zs_sem.at[side, t, h, r], zr_sem.at[side, t, h, r],
                      dev(y, c, x, at_z(1) if up else at_z(NZ - 1)))

    def z_halves(up, t):
        if t < 3:
            return (0, 1)
        return (0,) if up else (1,)

    def x_copy(q, h, e):
        t, up = SOURCES[q]
        zsrc = at_z(NZ - t) if up else at_z(t)
        rows = pl.ds(h * HALF, HALF)
        return remote(stage.at[q, e - 1, rows], pool.at[NF + x * NZ + zsrc, rows], xs_sem.at[q, h, e - 1],
                      xr_sem.at[q, h, e - 1], dev(y, c, at_x(e), z))

    def pick(q, h):
        t, up = SOURCES[q]
        zsrc = at_z(NZ - t) if up else at_z(t)
        rows = HALF // 2
        for e in (2, 1, 3):
            chosen = tab[PICK, e * NZ + zsrc]

            def part(i, carry):
                at = pl.ds(pl.multiple_of(h * HALF + i * rows, rows), rows)
                got = pool[zsrc * BR, at, :]
                for r in range(1, BR):
                    got = jnp.where(chosen == r, pool[zsrc * BR + r, at, :], got)
                stage[q, e - 1, at, :] = got
                return carry

            lax.fori_loop(0, 2, part, 0)
            x_copy(q, h, e).start()

    for r in range(BR):
        loads[r].wait()
    for h in range(2):
        for r in range(BR):
            z_copy(True, 0, h, r).start()
            z_copy(False, 0, h, r).start()
    for h in range(2):
        pick(0, h)

    def first(b, carry):
        block = jnp.where(tab[FILLED, b] > 0, prec[b], 0.0)
        turned = block.T
        wt[b] = turned.astype(BF16)
        tile[...] = jnp.where(tab[FLIP, b] > 0, turned, block)
        oc[b] = tile[pl.ds(pl.multiple_of(samp * CH, CH), CH), :]
        return carry

    for t in range(1, 5):
        for h in range(2):
            for r in range(BR):
                for up in (True, False):
                    if h in z_halves(up, t - 1):
                        z_copy(up, t - 1, h, r).wait_recv()
                        if t < 4 and h in z_halves(up, t):
                            z_copy(up, t, h, r).start()
            for q in range(len(SOURCES)):
                if SOURCES[q][0] == t:
                    pick(q, h)
            if t == 1 and h == 0:
                loads[BR].wait()
                lax.fori_loop(0, NBK, first, 0)
    for q in range(len(SOURCES)):
        for h in range(2):
            for e in range(1, NX):
                x_copy(q, h, e).wait_recv()
    for up in (True, False):
        for t in range(4):
            for h in z_halves(up, t):
                for r in range(BR):
                    z_copy(up, t, h, r).wait_send()
    for q in range(len(SOURCES)):
        for h in range(2):
            for e in range(1, NX):
                x_copy(q, h, e).wait_send()

    def gather_slots(b, carry):
        j, k = b // SL, b % SL
        stk[j, :, pl.ds(pl.multiple_of(k * BK, BK), BK)] = pool[tab[POOL, b]]
        return carry

    lax.fori_loop(0, NBK, gather_slots, 0)

    last = ITERS - 1

    def pair_copy(it, j):
        return remote(ub.at[it, j], sb.at[it, j], bs_sem.at[it, j], br_sem.at[it, j], dev(y, 1 - c, x, z))

    def y_copy(it, j, d):
        return remote(yb.at[it, j, d - 1], yr.at[it, j, d - 1], ys_sem.at[it, j, d - 1], yr_sem.at[it, j, d - 1],
                      dev(at_y(d), c, x, z))

    def pass_on(it, j):
        pair_copy(it, j).wait_recv()
        for d in (2, 1, 3, 0):
            yy = at_y(d)
            summed = uf[j, yy] + sb[it, j, yy].astype(F32)
            if d == 0:
                own[j] = summed
            else:
                yb[it, j, d - 1] = summed.astype(BF16)
                y_copy(it, j, d).start()

    def mirror_copy(it, i):
        e, d = i // NZ, i % NZ
        return remote(ms.at[it, i], mz.at[it, i], ms_sem.at[it, i], mr_sem.at[it, i], dev(y, c, at_x(e), at_z(d)))

    def far_first(n):
        kz, kx = n // NX, n % NX
        d = (NZ // 2 + (kz + 1) // 2 * (2 * (kz % 2) - 1)) % NZ
        e = (NX // 2 + (kx + 1) // 2 * (2 * (kx % 2) - 1)) % NX
        return e * NZ + d

    def piece_of(ref, j):
        return ref.at[pl.ds(pl.multiple_of(j * SL, SL), SL)]

    def gather_y(src, dst, it, j, d):
        return remote(piece_of(src, j), dst.at[j, samp], gs_sem.at[it, j, d - 1], gr_sem.at[it, j, d - 1],
                      dev(at_y(d), c, x, z))

    def gather_c(src, dst, it, j, e):
        holder = at_y(NY - e) * NC + c if e else samp
        source = dst.at[j, holder] if e else piece_of(src, j)
        return remote(source, dst.at[j, holder], hs_sem.at[it, j, e], hr_sem.at[it, j, e], dev(y, 1 - c, x, z))

    def gather_start(src, dst, it, j):
        for d in (2, 1, 3):
            gather_y(src, dst, it, j, d).start()
        gather_c(src, dst, it, j, 0).start()
        dst[j, samp] = src[pl.ds(pl.multiple_of(j * SL, SL), SL)]

    def gather_turn(src, dst, it, j):
        for d in (1, 3, 2):
            gather_y(src, dst, it, j, d).wait_recv()
            gather_c(src, dst, it, j, d).start()

    def gather_done(src, dst, it, j):
        for e in range(NY):
            gather_c(src, dst, it, j, e).wait_recv()

    def gather_sent(src, dst, it):
        def sent(j, carry):
            for d in range(1, NY):
                gather_y(src, dst, it, j, d).wait_send()
            for e in range(NY):
                gather_c(src, dst, it, j, e).wait_send()
            return carry

        lax.fori_loop(0, BR, sent, 0)

    def iteration(it, carry):
        @pl.when(it > 0)
        def _():
            gather_turn(wc.at[it - 1], wg.at[it - 1], it - 1, 0)

        def row(j, carry):
            @pl.when(it > 0)
            def _():
                gather_done(wc.at[it - 1], wg.at[it - 1], it - 1, j)
                for k in range(SL):
                    block = wg[it - 1, j, :, k].reshape(BK, BK)
                    wt[j * SL + k] = jnp.where(tab[FLIP, j * SL + k] > 0, block, block.T)

            part = ROWS // 4
            weights = wt[pl.ds(pl.multiple_of(j * SL, SL), SL)].reshape(SL * BK, BK)
            for i in range(4):
                projected = jnp.dot(stk[j, i * part:(i + 1) * part, :], weights, preferred_element_type=F32)
                yt[:, i * part:(i + 1) * part] = projected.astype(BF16).T
            vv[...] = jnp.dot(yt[...], stk[j], preferred_element_type=F32)

            @pl.when((it > 0) & (j < BR - 1))
            def _():
                gather_turn(wc.at[it - 1], wg.at[it - 1], it - 1, j + 1)

            for k in range(SL):
                block = vv[:, k * BK:(k + 1) * BK]
                turned = block.T
                if k == 0:
                    block = 0.5 * (block + turned)
                else:
                    block = jnp.where(tab[FLIP, j * SL + k] > 0, turned, block)
                cut = block.reshape(NY, NC, CH, BK)
                even, odd = cut[:, 0], cut[:, 1]
                uf[j, :, k] = jnp.where(c == 0, even, odd)
                ub[it, j, :, k] = jnp.where(c == 0, odd, even).astype(BF16)
            pair_copy(it, j).start()

            @pl.when(j > 0)
            def _():
                pass_on(it, j - 1)

            return carry

        lax.fori_loop(0, BR, row, 0)
        pass_on(it, BR - 1)

        def finish(j, carry):
            total = own[j]
            for d in range(1, NY):
                y_copy(it, j, d).wait_recv()
                total = total + yr[it, j, d - 1].astype(F32)
            uc[pl.ds(pl.multiple_of(j * SL, SL), SL)] = total
            return carry

        lax.fori_loop(0, BR, finish, 0)

        def post(n, carry):
            i = far_first(n)
            ms[it, i] = uc[tab[LINK, at_x(i // NZ) * NZ + at_z(i % NZ)]].astype(BF16)
            mirror_copy(it, i).start()
            return carry

        lax.fori_loop(0, NF - 1, post, 0)

        def collect(n, carry):
            i = far_first(n)
            mirror_copy(it, i).wait_recv()
            mloc[at_z(NZ - i % NZ), at_x(NX - i // NZ)] = mz[it, i]
            return carry

        lax.fori_loop(0, NF - 1, collect, 0)

        def update(j, carry):
            for k in range(SL):
                b = j * SL + k
                gradient = uc[b]
                if k > 0:
                    peer = tab[PEER, b]
                    mirrored = jnp.where(tab[LOCAL, b] > 0, uc[tab[MATE, b]], mloc[peer // NX, peer % NX].astype(F32))
                    gradient = 0.5 * (gradient + mirrored)
                stepped = oc[b] - STEP * (gradient * (1.0 / (ROWS * NS)))
                result = jnp.where(stepped > 0, jnp.maximum(stepped - SHRINK, 0.0), jnp.minimum(stepped + SHRINK, 0.0))
                if k == 0:
                    rooted = 0.5 * (stepped + jnp.sqrt(stepped * stepped + 4.0 * STEP))
                    across = lax.broadcasted_iota(jnp.int32, (CH, BK), 1)
                    down = lax.broadcasted_iota(jnp.int32, (CH, BK), 0) + samp * CH
                    result = jnp.where(across == down, rooted, result)
                result = jnp.where(tab[FILLED, b] > 0, result, 0.0)
                oc[b] = result
                wc[it, b] = result.astype(BF16)

            @pl.when(it < last)
            def _():
                gather_start(wc.at[it], wg.at[it], it, j)

            @pl.when(it == last)
            def _():
                gather_start(oc, og, last, j)

            return carry

        lax.fori_loop(0, BR, update, 0)
        return carry

    lax.fori_loop(0, ITERS, iteration, 0)

    def out_copy(j):
        rows = pl.ds(pl.multiple_of(j * SL, SL), SL)
        return pltpu.make_async_copy(result_rows.at[rows], out_hbm.at[rows], out_sem.at[j])

    gather_turn(oc, og, last, 0)

    def store(j, carry):
        gather_done(oc, og, last, j)
        for k in range(SL):
            block = og[j, :, k].reshape(BK, BK)
            result_rows[j * SL + k] = jnp.where(tab[FLIP, j * SL + k] > 0, block.T, block)
        out_copy(j).start()

        @pl.when(j < BR - 1)
        def _():
            gather_turn(oc, og, last, j + 1)

        return carry

    lax.fori_loop(0, BR, store, 0)

    def sent(it, carry):
        for j in range(BR):
            pair_copy(it, j).wait_send()
            for d in range(1, NY):
                y_copy(it, j, d).wait_send()

        def mirror_sent(i, carry):
            mirror_copy(it, i).wait_send()
            return carry

        lax.fori_loop(1, NF, mirror_sent, 0)

        @pl.when(it < last)
        def _():
            gather_sent(wc.at[it], wg.at[it], it)

        return carry

    lax.fori_loop(0, ITERS, sent, 0)
    gather_sent(oc, og, last)
    for j in range(BR):
        out_copy(j).wait()


def tables(col_blocks):
    feat = lax.axis_index("feat")
    cols = col_blocks.reshape(NBK)
    filled = cols >= 0
    place = jnp.arange(NBK, dtype=jnp.int32)
    row_ids = feat * BR + place // SL
    holder = jnp.where(filled, cols // BR, feat)
    inside = jnp.where(filled, cols % BR, 0)
    hx, hz = holder // NZ, holder % NZ
    same_x = hx == feat // NZ
    pool = jnp.where(same_x, hz * BR + inside, NF + holder)
    flip = filled & (cols < row_ids)
    local = filled & (holder == feat)
    pair = (cols[:, None] == row_ids[None, :]) & (cols[None, :] == row_ids[:, None])
    mate = jnp.sum(jnp.where(pair, place[None, :], 0), axis=1)
    linked = (filled & (holder != feat))[None, :] & (holder[None, :] == jnp.arange(NF, dtype=jnp.int32)[:, None])
    link = jnp.sum(jnp.where(linked, place[None, :], 0), axis=1)
    rows = jnp.sum(jnp.where(linked, inside[None, :], 0), axis=1)
    outgoing = lax.dynamic_slice(jnp.concatenate([rows, rows]), ((feat // NZ) * NZ,), (NF,)).reshape(NX, NZ)
    come = [lax.ppermute(outgoing[NX - e], "feat", [(xx * NZ + zz, (xx + NX - e) % NX * NZ + zz) for xx in range(NX)
                                                    for zz in range(NZ)]) for e in range(1, NX)]
    picks = jnp.concatenate([outgoing[0]] + come)
    scalars = [pool, flip.astype(jnp.int32), local.astype(jnp.int32), mate, hz * NX + hx, filled.astype(jnp.int32), link, picks]
    return jnp.concatenate(scalars).reshape(8, NBK)


def local(samples, precision, col_blocks):
    anywhere = pl.BlockSpec(memory_space=pl.ANY)
    piece = (SL, CH, BK)
    dma = pltpu.SemaphoreType.DMA
    result = pl.pallas_call(
        kernel,
        out_shape=jax.ShapeDtypeStruct((NBK, BK, BK), F32),
        in_specs=[pl.BlockSpec(memory_space=pltpu.SMEM), anywhere, anywhere],
        out_specs=anywhere,
        scratch_shapes=[
            pltpu.VMEM((2 * NF, ROWS, BK), BF16),
            pltpu.VMEM((NZ, 3, ROWS, BK), BF16),
            pltpu.VMEM((BR, ROWS, SL * BK), BF16),
            pltpu.VMEM((NBK, BK, BK), BF16),
            pltpu.VMEM((BK, ROWS), BF16),
            pltpu.VMEM((BK, SL * BK), F32),
            pltpu.VMEM((BK, BK), F32),
            pltpu.VMEM((NBK, BK, BK), F32),
            pltpu.VMEM((NBK, CH, BK), F32),
            pltpu.VMEM((ITERS, BR, NY) + piece, BF16),
            pltpu.VMEM((BR, NY) + piece, F32),
            pltpu.VMEM((ITERS, BR, NY) + piece, BF16),
            pltpu.VMEM((BR,) + piece, F32),
            pltpu.VMEM((ITERS, BR, NY - 1) + piece, BF16),
            pltpu.VMEM((ITERS, BR, NY - 1) + piece, BF16),
            pltpu.VMEM((NBK, CH, BK), F32),
            pltpu.VMEM((ITERS, NF, CH, BK), BF16),
            pltpu.VMEM((ITERS, NF, CH, BK), BF16),
            pltpu.VMEM((NZ, NX, CH, BK), BF16),
            pltpu.VMEM((ITERS, NBK, CH, BK), BF16),
            pltpu.VMEM((ITERS - 1, BR, NS) + piece, BF16),
            pltpu.VMEM((BR, NS) + piece, F32),
            pltpu.VMEM((NBK, BK, BK), F32),
            dma((BR + 1,)), dma((BR,)),
            dma((2, 4, 2, BR)), dma((2, 4, 2, BR)),
            dma((NZ, 2, NX - 1)), dma((NZ, 2, NX - 1)),
            dma((ITERS, BR)), dma((ITERS, BR)),
            dma((ITERS, BR, NY - 1)), dma((ITERS, BR, NY - 1)),
            dma((ITERS, NF)), dma((ITERS, NF)),
            dma((ITERS, BR, NY - 1)), dma((ITERS, BR, NY - 1)),
            dma((ITERS, BR, NY)), dma((ITERS, BR, NY)),
        ],
        compiler_params=pltpu.CompilerParams(collective_id=0, has_side_effects=True, vmem_limit_bytes=60 * 2**20),
        name="prox_iterations",
    )(tables(col_blocks), samples, precision.reshape(NBK, BK, BK))
    return result.reshape(BR, SL, BK, BK)


def solution(mesh):
    if mesh.shape["samp"] != NS or mesh.shape["feat"] != NF:
        raise ValueError("unexpected mesh")
    return jax.shard_map(
        local,
        mesh=mesh,
        in_specs=(P("samp", "feat"), P("feat", None, None, None), P("feat", None)),
        out_specs=P("feat", None, None, None),
        check_vma=False,
    )
```

```python
import functools

import jax
import jax.numpy as jnp
from jax import lax
from jax.experimental import pallas as pl
from jax.experimental.pallas import tpu as pltpu
from jax.sharding import PartitionSpec as P

ITERS = 3
STEP = 0.2
SHRINK = 0.2 * 0.25
NX, NZ, NY, NC = 4, 8, 4, 2
NS = NY * NC
NF = NX * NZ
BR, SL, BK = 4, 8, 128
NBK = BR * SL
CH = BK // NS
ROWS = 1024
F32, BF16 = jnp.float32, jnp.bfloat16
MESH = pl.DeviceIdType.MESH

PIECES = 4
HALF = ROWS // PIECES

POOL, FLIP, LOCAL, MATE, PEER, FILLED, LINK, PICK = range(8)
SOURCES = ((0, True), (1, True), (1, False), (2, True), (2, False), (3, True), (3, False), (4, True))


def kernel(tab, x_hbm, prec_hbm, out_hbm, pool, stage, stk, wt, yt, vv, tile, prec, oc,
           ub, uf, sb, own, yb, yr, uc, ms, mz, mloc, wc, wg, og, result_rows, loc_sem, out_sem,
           zs_sem, zr_sem, xs_sem, xr_sem, bs_sem, br_sem, ys_sem, yr_sem, ms_sem, mr_sem, gs_sem, gr_sem,
           hs_sem, hr_sem):
    samp, feat = lax.axis_index("samp"), lax.axis_index("feat")
    y, c = samp // NC, samp % NC
    x, z = feat // NZ, feat % NZ

    def at_x(d):
        return (x + d) % NX

    def at_z(d):
        return (z + d) % NZ

    def at_y(d):
        return (y + d) % NY

    def dev(yy, cc, xx, zz):
        return (yy * NC + cc, xx * NZ + zz)

    def remote(src, dst, ssem, rsem, device):
        return pltpu.make_async_remote_copy(src_ref=src, dst_ref=dst, send_sem=ssem, recv_sem=rsem, device_id=device,
                                            device_id_type=MESH)

    barrier = pltpu.get_barrier_semaphore()
    peers = ([dev(y, c, at_x(i // NZ), at_z(i % NZ)) for i in range(1, NF)]
             + [dev(at_y(d), c, x, z) for d in range(1, NY)] + [dev(y, 1 - c, x, z)])
    for peer in peers:
        pl.semaphore_signal(barrier, inc=1, device_id=peer, device_id_type=MESH)
    loads = [pltpu.make_async_copy(x_hbm.at[:, pl.ds(r * BK, BK)], pool.at[z * BR + r], loc_sem.at[r]) for r in range(BR)]
    loads.append(pltpu.make_async_copy(prec_hbm, prec, loc_sem.at[BR]))
    for load in loads:
        load.start()
    pl.semaphore_wait(barrier, len(peers))

    def z_copy(up, t, h, r):
        source = at_z(NZ - t) if up else at_z(t)
        piece = pool.at[source * BR + r, pl.ds(h * HALF, HALF)]
        side = 0 if up else 1
        return remote(piece, piece, zs_sem.at[side, t, h, r], zr_sem.at[side, t, h, r],
                      dev(y, c, x, at_z(1) if up else at_z(NZ - 1)))

    def z_halves(up, t):
        if t < 3:
            return range(PIECES)
        return range(0, PIECES // 2) if up else range(PIECES // 2, PIECES)

    def x_copy(q, h, e):
        t, up = SOURCES[q]
        zsrc = at_z(NZ - t) if up else at_z(t)
        rows = pl.ds(h * HALF, HALF)
        return remote(stage.at[q, e - 1, rows], pool.at[NF + x * NZ + zsrc, rows], xs_sem.at[q, h, e - 1],
                      xr_sem.at[q, h, e - 1], dev(y, c, at_x(e), z))

    def pick(q, h):
        t, up = SOURCES[q]
        zsrc = at_z(NZ - t) if up else at_z(t)
        rows = HALF // 2
        for e in (2, 1, 3):
            chosen = tab[PICK, e * NZ + zsrc]

            def part(i, carry):
                at = pl.ds(pl.multiple_of(h * HALF + i * rows, rows), rows)
                got = pool[zsrc * BR, at, :]
                for r in range(1, BR):
                    got = jnp.where(chosen == r, pool[zsrc * BR + r, at, :], got)
                stage[q, e - 1, at, :] = got
                return carry

            lax.fori_loop(0, 2, part, 0)
            x_copy(q, h, e).start()

    for r in range(BR):
        loads[r].wait()
    for h in range(PIECES):
        for r in range(BR):
            z_copy(True, 0, h, r).start()
            z_copy(False, 0, h, r).start()
    for h in range(PIECES):
        pick(0, h)

    def first(b, carry):
        block = jnp.where(tab[FILLED, b] > 0, prec[b], 0.0)
        turned = block.T
        wt[b] = turned.astype(BF16)
        tile[...] = jnp.where(tab[FLIP, b] > 0, turned, block)
        oc[b] = tile[pl.ds(pl.multiple_of(samp * CH, CH), CH), :]
        return carry

    for t in range(1, 5):
        for h in range(PIECES):
            for r in range(BR):
                for up in (True, False):
                    if h in z_halves(up, t - 1):
                        z_copy(up, t - 1, h, r).wait_recv()
                        if t < 4 and h in z_halves(up, t):
                            z_copy(up, t, h, r).start()
            for q in range(len(SOURCES)):
                if SOURCES[q][0] == t:
                    pick(q, h)
            if t == 1 and h == 0:
                loads[BR].wait()
                lax.fori_loop(0, NBK, first, 0)
    for q in range(len(SOURCES)):
        for h in range(PIECES):
            for e in range(1, NX):
                x_copy(q, h, e).wait_recv()
    for up in (True, False):
        for t in range(4):
            for h in z_halves(up, t):
                for r in range(BR):
                    z_copy(up, t, h, r).wait_send()
    for q in range(len(SOURCES)):
        for h in range(PIECES):
            for e in range(1, NX):
                x_copy(q, h, e).wait_send()

    def gather_slots(b, carry):
        j, k = b // SL, b % SL
        stk[j, :, pl.ds(pl.multiple_of(k * BK, BK), BK)] = pool[tab[POOL, b]]
        return carry

    lax.fori_loop(0, NBK, gather_slots, 0)

    last = ITERS - 1

    def pair_copy(it, j):
        return remote(ub.at[it, j], sb.at[it, j], bs_sem.at[it, j], br_sem.at[it, j], dev(y, 1 - c, x, z))

    def y_copy(it, j, d):
        return remote(yb.at[it, j, d - 1], yr.at[it, j, d - 1], ys_sem.at[it, j, d - 1], yr_sem.at[it, j, d - 1],
                      dev(at_y(d), c, x, z))

    def pass_on(it, j):
        pair_copy(it, j).wait_recv()
        for d in (2, 1, 3, 0):
            yy = at_y(d)
            summed = uf[j, yy] + sb[it, j, yy].astype(F32)
            if d == 0:
                own[j] = summed
            else:
                yb[it, j, d - 1] = summed.astype(BF16)
                y_copy(it, j, d).start()

    def mirror_copy(it, i):
        e, d = i // NZ, i % NZ
        return remote(ms.at[it, i], mz.at[it, i], ms_sem.at[it, i], mr_sem.at[it, i], dev(y, c, at_x(e), at_z(d)))

    def far_first(n):
        kz, kx = n // NX, n % NX
        d = (NZ // 2 + (kz + 1) // 2 * (2 * (kz % 2) - 1)) % NZ
        e = (NX // 2 + (kx + 1) // 2 * (2 * (kx % 2) - 1)) % NX
        return e * NZ + d

    def piece_of(ref, j):
        return ref.at[pl.ds(pl.multiple_of(j * SL, SL), SL)]

    def gather_y(src, dst, it, j, d):
        return remote(piece_of(src, j), dst.at[j, samp], gs_sem.at[it, j, d - 1], gr_sem.at[it, j, d - 1],
                      dev(at_y(d), c, x, z))

    def gather_c(src, dst, it, j, e):
        holder = at_y(NY - e) * NC + c if e else samp
        source = dst.at[j, holder] if e else piece_of(src, j)
        return remote(source, dst.at[j, holder], hs_sem.at[it, j, e], hr_sem.at[it, j, e], dev(y, 1 - c, x, z))

    def gather_start(src, dst, it, j):
        for d in (2, 1, 3):
            gather_y(src, dst, it, j, d).start()
        gather_c(src, dst, it, j, 0).start()
        dst[j, samp] = src[pl.ds(pl.multiple_of(j * SL, SL), SL)]

    def gather_turn(src, dst, it, j):
        for d in (1, 3, 2):
            gather_y(src, dst, it, j, d).wait_recv()
            gather_c(src, dst, it, j, d).start()

    def gather_done(src, dst, it, j):
        for e in range(NY):
            gather_c(src, dst, it, j, e).wait_recv()

    def gather_sent(src, dst, it):
        def sent(j, carry):
            for d in range(1, NY):
                gather_y(src, dst, it, j, d).wait_send()
            for e in range(NY):
                gather_c(src, dst, it, j, e).wait_send()
            return carry

        lax.fori_loop(0, BR, sent, 0)

    def iteration(it, carry):
        @pl.when(it > 0)
        def _():
            gather_turn(wc.at[it - 1], wg.at[it - 1], it - 1, 0)

        def row(j, carry):
            @pl.when(it > 0)
            def _():
                gather_done(wc.at[it - 1], wg.at[it - 1], it - 1, j)
                for k in range(SL):
                    block = wg[it - 1, j, :, k].reshape(BK, BK)
                    wt[j * SL + k] = jnp.where(tab[FLIP, j * SL + k] > 0, block, block.T)

            part = ROWS // 4
            weights = wt[pl.ds(pl.multiple_of(j * SL, SL), SL)].reshape(SL * BK, BK)
            for i in range(4):
                projected = jnp.dot(stk[j, i * part:(i + 1) * part, :], weights, preferred_element_type=F32)
                yt[:, i * part:(i + 1) * part] = projected.astype(BF16).T
            vv[...] = jnp.dot(yt[...], stk[j], preferred_element_type=F32)

            @pl.when((it > 0) & (j < BR - 1))
            def _():
                gather_turn(wc.at[it - 1], wg.at[it - 1], it - 1, j + 1)

            for k in range(SL):
                block = vv[:, k * BK:(k + 1) * BK]
                turned = block.T
                if k == 0:
                    block = 0.5 * (block + turned)
                else:
                    block = jnp.where(tab[FLIP, j * SL + k] > 0, turned, block)
                cut = block.reshape(NY, NC, CH, BK)
                even, odd = cut[:, 0], cut[:, 1]
                uf[j, :, k] = jnp.where(c == 0, even, odd)
                ub[it, j, :, k] = jnp.where(c == 0, odd, even).astype(BF16)
            pair_copy(it, j).start()

            @pl.when(j > 0)
            def _():
                pass_on(it, j - 1)

            return carry

        lax.fori_loop(0, BR, row, 0)
        pass_on(it, BR - 1)

        def finish(j, carry):
            total = own[j]
            for d in range(1, NY):
                y_copy(it, j, d).wait_recv()
                total = total + yr[it, j, d - 1].astype(F32)
            uc[pl.ds(pl.multiple_of(j * SL, SL), SL)] = total
            return carry

        lax.fori_loop(0, BR, finish, 0)

        def post(n, carry):
            i = far_first(n)
            ms[it, i] = uc[tab[LINK, at_x(i // NZ) * NZ + at_z(i % NZ)]].astype(BF16)
            mirror_copy(it, i).start()
            return carry

        lax.fori_loop(0, NF - 1, post, 0)

        def collect(n, carry):
            i = far_first(n)
            mirror_copy(it, i).wait_recv()
            mloc[at_z(NZ - i % NZ), at_x(NX - i // NZ)] = mz[it, i]
            return carry

        lax.fori_loop(0, NF - 1, collect, 0)

        def update(j, carry):
            for k in range(SL):
                b = j * SL + k
                gradient = uc[b]
                if k > 0:
                    peer = tab[PEER, b]
                    mirrored = jnp.where(tab[LOCAL, b] > 0, uc[tab[MATE, b]], mloc[peer // NX, peer % NX].astype(F32))
                    gradient = 0.5 * (gradient + mirrored)
                stepped = oc[b] - STEP * (gradient * (1.0 / (ROWS * NS)))
                result = jnp.where(stepped > 0, jnp.maximum(stepped - SHRINK, 0.0), jnp.minimum(stepped + SHRINK, 0.0))
                if k == 0:
                    rooted = 0.5 * (stepped + jnp.sqrt(stepped * stepped + 4.0 * STEP))
                    across = lax.broadcasted_iota(jnp.int32, (CH, BK), 1)
                    down = lax.broadcasted_iota(jnp.int32, (CH, BK), 0) + samp * CH
                    result = jnp.where(across == down, rooted, result)
                result = jnp.where(tab[FILLED, b] > 0, result, 0.0)
                oc[b] = result
                wc[it, b] = result.astype(BF16)

            @pl.when(it < last)
            def _():
                gather_start(wc.at[it], wg.at[it], it, j)

            @pl.when(it == last)
            def _():
                gather_start(oc, og, last, j)

            return carry

        lax.fori_loop(0, BR, update, 0)
        return carry

    lax.fori_loop(0, ITERS, iteration, 0)

    def out_copy(j):
        rows = pl.ds(pl.multiple_of(j * SL, SL), SL)
        return pltpu.make_async_copy(result_rows.at[rows], out_hbm.at[rows], out_sem.at[j])

    gather_turn(oc, og, last, 0)

    def store(j, carry):
        gather_done(oc, og, last, j)
        for k in range(SL):
            block = og[j, :, k].reshape(BK, BK)
            result_rows[j * SL + k] = jnp.where(tab[FLIP, j * SL + k] > 0, block.T, block)
        out_copy(j).start()

        @pl.when(j < BR - 1)
        def _():
            gather_turn(oc, og, last, j + 1)

        return carry

    lax.fori_loop(0, BR, store, 0)

    def sent(it, carry):
        for j in range(BR):
            pair_copy(it, j).wait_send()
            for d in range(1, NY):
                y_copy(it, j, d).wait_send()

        def mirror_sent(i, carry):
            mirror_copy(it, i).wait_send()
            return carry

        lax.fori_loop(1, NF, mirror_sent, 0)

        @pl.when(it < last)
        def _():
            gather_sent(wc.at[it], wg.at[it], it)

        return carry

    lax.fori_loop(0, ITERS, sent, 0)
    gather_sent(oc, og, last)
    for j in range(BR):
        out_copy(j).wait()


def tables(col_blocks):
    feat = lax.axis_index("feat")
    cols = col_blocks.reshape(NBK)
    filled = cols >= 0
    place = jnp.arange(NBK, dtype=jnp.int32)
    row_ids = feat * BR + place // SL
    holder = jnp.where(filled, cols // BR, feat)
    inside = jnp.where(filled, cols % BR, 0)
    hx, hz = holder // NZ, holder % NZ
    same_x = hx == feat // NZ
    pool = jnp.where(same_x, hz * BR + inside, NF + holder)
    flip = filled & (cols < row_ids)
    local = filled & (holder == feat)
    pair = (cols[:, None] == row_ids[None, :]) & (cols[None, :] == row_ids[:, None])
    mate = jnp.sum(jnp.where(pair, place[None, :], 0), axis=1)
    linked = (filled & (holder != feat))[None, :] & (holder[None, :] == jnp.arange(NF, dtype=jnp.int32)[:, None])
    link = jnp.sum(jnp.where(linked, place[None, :], 0), axis=1)
    rows = jnp.sum(jnp.where(linked, inside[None, :], 0), axis=1)
    outgoing = lax.dynamic_slice(jnp.concatenate([rows, rows]), ((feat // NZ) * NZ,), (NF,)).reshape(NX, NZ)
    come = [lax.ppermute(outgoing[NX - e], "feat", [(xx * NZ + zz, (xx + NX - e) % NX * NZ + zz) for xx in range(NX)
                                                    for zz in range(NZ)]) for e in range(1, NX)]
    picks = jnp.concatenate([outgoing[0]] + come)
    scalars = [pool, flip.astype(jnp.int32), local.astype(jnp.int32), mate, hz * NX + hx, filled.astype(jnp.int32), link, picks]
    return jnp.concatenate(scalars).reshape(8, NBK)


def local(samples, precision, col_blocks):
    anywhere = pl.BlockSpec(memory_space=pl.ANY)
    piece = (SL, CH, BK)
    dma = pltpu.SemaphoreType.DMA
    result = pl.pallas_call(
        kernel,
        out_shape=jax.ShapeDtypeStruct((NBK, BK, BK), F32),
        in_specs=[pl.BlockSpec(memory_space=pltpu.SMEM), anywhere, anywhere],
        out_specs=anywhere,
        scratch_shapes=[
            pltpu.VMEM((2 * NF, ROWS, BK), BF16),
            pltpu.VMEM((NZ, 3, ROWS, BK), BF16),
            pltpu.VMEM((BR, ROWS, SL * BK), BF16),
            pltpu.VMEM((NBK, BK, BK), BF16),
            pltpu.VMEM((BK, ROWS), BF16),
            pltpu.VMEM((BK, SL * BK), F32),
            pltpu.VMEM((BK, BK), F32),
            pltpu.VMEM((NBK, BK, BK), F32),
            pltpu.VMEM((NBK, CH, BK), F32),
            pltpu.VMEM((ITERS, BR, NY) + piece, BF16),
            pltpu.VMEM((BR, NY) + piece, F32),
            pltpu.VMEM((ITERS, BR, NY) + piece, BF16),
            pltpu.VMEM((BR,) + piece, F32),
            pltpu.VMEM((ITERS, BR, NY - 1) + piece, BF16),
            pltpu.VMEM((ITERS, BR, NY - 1) + piece, BF16),
            pltpu.VMEM((NBK, CH, BK), F32),
            pltpu.VMEM((ITERS, NF, CH, BK), BF16),
            pltpu.VMEM((ITERS, NF, CH, BK), BF16),
            pltpu.VMEM((NZ, NX, CH, BK), BF16),
            pltpu.VMEM((ITERS, NBK, CH, BK), BF16),
            pltpu.VMEM((ITERS - 1, BR, NS) + piece, BF16),
            pltpu.VMEM((BR, NS) + piece, F32),
            pltpu.VMEM((NBK, BK, BK), F32),
            dma((BR + 1,)), dma((BR,)),
            dma((2, 4, PIECES, BR)), dma((2, 4, PIECES, BR)),
            dma((NZ, PIECES, NX - 1)), dma((NZ, PIECES, NX - 1)),
            dma((ITERS, BR)), dma((ITERS, BR)),
            dma((ITERS, BR, NY - 1)), dma((ITERS, BR, NY - 1)),
            dma((ITERS, NF)), dma((ITERS, NF)),
            dma((ITERS, BR, NY - 1)), dma((ITERS, BR, NY - 1)),
            dma((ITERS, BR, NY)), dma((ITERS, BR, NY)),
        ],
        compiler_params=pltpu.CompilerParams(collective_id=0, has_side_effects=True, vmem_limit_bytes=60 * 2**20),
        name="prox_iterations",
    )(tables(col_blocks), samples, precision.reshape(NBK, BK, BK))
    return result.reshape(BR, SL, BK, BK)


def solution(mesh):
    if mesh.shape["samp"] != NS or mesh.shape["feat"] != NF:
        raise ValueError("unexpected mesh")
    return jax.shard_map(
        local,
        mesh=mesh,
        in_specs=(P("samp", "feat"), P("feat", None, None, None), P("feat", None)),
        out_specs=P("feat", None, None, None),
        check_vma=False,
    )
```
